768 devices in a mesh: ctx: 96 (over x, z, core), head: 8 (over y).
Axes of the slice: x: 4, y: 8, z: 12, core: 2. Of those that a mesh axis runs over, the one named last changes fastest.
Arguments:
- queries: bfloat16 [24576, 4096], P('ctx', 'head'), may hold values from -64 to 64
- key_vectors: bfloat16 [24576, 1024], P('ctx', 'head'), may hold values from -4.5 to 4.5
- value_vectors: bfloat16 [24576, 1024], P('ctx', 'head'), may hold values from -6 to 6
- out_weight: bfloat16 [4096, 4096], P('head'), may hold values from -0.09375 to 0.09375
- offsets: int32 [25], replicated, may hold values from 0 to 24576, as said below
Outputs:
- projected: bfloat16 [4096, 24576], P('head', 'ctx')
The draws below stay inside these ranges and needn't reach their ends.
Inputs may be any that keep to these rules, and one draw needn't show every extreme that they name: offsets[0] = 0 and offsets[24] = 24576; offsets rise strictly; every document has 1 to 3840 tokens and one has exactly 3840.
All inputs are finite; a program needn't handle non-finite values.
Results may differ from the reference program's by a relative error of at most 0.014.
Values may be sent and summed in bfloat16 or wider, within the bound.
A program may use at most 32 MiB of HBM per device.

```python
import jax
import jax.numpy as jnp
from jax import lax

D = 4096
HEADS = 32
KV_HEADS = 8
HEAD_DIM = 128
TOK_DEV = 256
TOKENS = 24576
MAXDOC = 3840
NDOCS = 24
N_HEAD = 8


def drawn_keys(key):
    kv_columns = KV_HEADS * HEAD_DIM
    return jnp.clip(jax.random.normal(key, (TOKENS, kv_columns), jnp.float32), -4.5, 4.5)


def drawn_pair(key):
    key_seed = jax.random.fold_in(key, 11)
    keys_drawn = drawn_keys(key_seed)
    return keys_drawn


def draw_queries(key, part):
    query_columns = HEADS * HEAD_DIM
    query_seed = jax.random.fold_in(key, 21)
    query_draw = jnp.clip(2.5 * jax.random.normal(query_seed, (TOKENS, query_columns), jnp.float32), -12.0, 12.0)
    return query_draw.astype(jnp.bfloat16)


def draw_key_vectors(key, part):
    keys_drawn = drawn_pair(key)
    return keys_drawn.astype(jnp.bfloat16)


def draw_offsets(key, part):
    others = NDOCS - 1
    remaining = TOKENS - MAXDOC
    base_length = remaining // others
    leftover = remaining - base_length * others
    positions = jnp.arange(others, dtype=jnp.int32)
    lengths = base_length + (positions < leftover).astype(jnp.int32)
    pair_count = others // 2
    nudges = jax.random.randint(jax.random.fold_in(key, 31), (pair_count,), -(base_length - 1), base_length).astype(jnp.int32)
    nudge_signed = jnp.zeros((others,), jnp.int32)
    nudge_signed = nudge_signed.at[0:2 * pair_count:2].set(nudges)
    nudge_signed = nudge_signed.at[1:2 * pair_count:2].set(-nudges)
    lengths = lengths + nudge_signed
    long_index = jax.random.randint(jax.random.fold_in(key, 32), (), 0, NDOCS).astype(jnp.int32)
    slots = jnp.arange(NDOCS, dtype=jnp.int32)
    before = lengths[jnp.minimum(slots, others - 1)]
    after = lengths[jnp.maximum(slots - 1, 0)]
    all_lengths = jnp.where(slots < long_index, before, jnp.where(slots == long_index, MAXDOC, after)).astype(jnp.int32)
    return jnp.concatenate([jnp.zeros((1,), jnp.int32), jnp.cumsum(all_lengths).astype(jnp.int32)])


def steps_of(key, shape, split, low, largest):
    level = 1.0
    for axis_at, blocks in split:
        draws = jax.random.uniform(jax.random.fold_in(jax.random.fold_in(key, 6), axis_at), (blocks,), jnp.float32, low / len(split), largest / len(split))
        level = level * jnp.repeat(jnp.exp(draws), shape[axis_at] // blocks).reshape((-1,) + (1,) * (len(shape) - 1 - axis_at))
    return level


def normal_values(rng, extent, deviation, limit, cuts=(), kind=jnp.bfloat16):
    array = jax.random.normal(rng, extent, jnp.float32) * deviation
    if len(cuts) > 0:
        array = steps_of(rng, extent, cuts, -0.22, 0.18) * array
    return jnp.clip(array, min=-limit, max=limit).astype(kind)


def setup_inputs(seed: int = 0) -> dict:
    streams_of = jax.random.split(jax.random.key(seed), 6)
    return {
        "queries": draw_queries(jax.random.fold_in(streams_of[5], 71), 0),
        "key_vectors": draw_key_vectors(jax.random.fold_in(streams_of[5], 71), 0),
        "value_vectors": normal_values(streams_of[2], (TOKENS, KV_HEADS * HEAD_DIM), 1.0, 6.0, ((0, 96), (1, 8))),
        "out_weight": normal_values(streams_of[3], (HEADS * HEAD_DIM, D), (HEADS * HEAD_DIM) ** -0.5, 0.09375, ((0, 8),)),
        "offsets": draw_offsets(jax.random.fold_in(streams_of[5], 71), 0),
    }


def doc_index(positions, offsets):
    boundaries = offsets[1:-1]
    return jnp.sum((positions[:, None] >= boundaries[None, :]).astype(jnp.int32), axis=1)


def reference(queries, key_vectors, value_vectors, out_weight, offsets):
    group_size = HEADS // KV_HEADS
    logit_scale = HEAD_DIM ** -0.5
    window = MAXDOC
    padding = jnp.zeros((window, KV_HEADS * HEAD_DIM), key_vectors.dtype)
    padded_keys = jnp.concatenate([padding, key_vectors], axis=0)
    padded_values = jnp.concatenate([padding, value_vectors], axis=0)

    def attend_block(block_index):
        row_start = (block_index * TOK_DEV).astype(jnp.int32)
        query_tile_rows = lax.dynamic_slice_in_dim(queries, row_start, TOK_DEV, 0).astype(jnp.float32)
        query_tile_rows = query_tile_rows.reshape(TOK_DEV, KV_HEADS, group_size, HEAD_DIM)
        key_tile_rows = lax.dynamic_slice_in_dim(padded_keys, row_start, window + TOK_DEV, 0).astype(jnp.float32)
        key_tile_rows = key_tile_rows.reshape(window + TOK_DEV, KV_HEADS, HEAD_DIM)
        value_tile_rows = lax.dynamic_slice_in_dim(padded_values, row_start, window + TOK_DEV, 0).astype(jnp.float32)
        value_tile_rows = value_tile_rows.reshape(window + TOK_DEV, KV_HEADS, HEAD_DIM)
        query_pos = row_start + jnp.arange(TOK_DEV, dtype=jnp.int32)
        key_pos = row_start - window + jnp.arange(window + TOK_DEV, dtype=jnp.int32)
        query_doc = doc_index(query_pos, offsets)
        key_doc = doc_index(key_pos, offsets)
        visible = (key_pos[None, :] >= 0) & (key_pos[None, :] <= query_pos[:, None]) & (key_doc[None, :] == query_doc[:, None])
        attention_logits = jnp.einsum("myqe,cye->yqmc", query_tile_rows, key_tile_rows) * logit_scale
        attention_logits = jnp.where(visible, attention_logits, -jnp.inf)
        row_max = jnp.max(attention_logits, axis=-1, keepdims=True)
        exponent = jnp.exp(attention_logits - row_max)
        row_sum = jnp.sum(exponent, axis=-1)
        attention_probs = lax.optimization_barrier(exponent.astype(jnp.bfloat16)).astype(jnp.float32)
        weighted_values = jnp.einsum("avmk,kab->mavb", attention_probs, value_tile_rows)
        attended = weighted_values / jnp.transpose(row_sum, (2, 0, 1))[..., None]
        return attended.reshape(TOK_DEV, HEADS * HEAD_DIM).astype(jnp.bfloat16)

    attended = lax.map(attend_block, jnp.arange(TOKENS // TOK_DEV, dtype=jnp.int32))
    attended = attended.reshape(TOKENS, HEADS * HEAD_DIM)
    group_cols = HEADS * HEAD_DIM // N_HEAD

    def add_group(group_index, accumulated):
        first_col = (group_index * group_cols).astype(jnp.int32)
        attended_cols = lax.dynamic_slice_in_dim(attended, first_col, group_cols, 1)
        weight_rows = lax.dynamic_slice_in_dim(out_weight, first_col, group_cols, 0)
        partial_value = jnp.dot(attended_cols, weight_rows, preferred_element_type=jnp.float32).astype(jnp.bfloat16)
        partial_value = lax.optimization_barrier(partial_value)
        return accumulated + partial_value.astype(jnp.float32)

    summed = lax.fori_loop(0, N_HEAD, add_group, jnp.zeros((TOKENS, D), jnp.float32))
    return jnp.transpose(summed).astype(jnp.bfloat16)
```

```python
import functools
import math

import jax
import jax.numpy as jnp
from jax import lax
from jax.experimental import pallas as pl
from jax.experimental.pallas import tpu as pltpu
from jax.sharding import PartitionSpec as P

HEAD_DIM = 128
LAST = 7
MESH = pl.DeviceIdType.MESH
NEG = -1e30
UNSEEN = -(1 << 24)

CHAINS = ((4, 1, -1, 0), (4, -1, 1, 1), (5, 1, -1, 1), (3, -1, 1, 0))


def stops(chain):
    first, step, _, _ = CHAINS[chain]
    return [r % 8 for r in range(first, 8 if step == 1 else 0, step)]


def kernel(
    n_ctx, n_head, offsets_ref, q_hbm, k_hbm, v_hbm, w_hbm, out_ref,
    kv, q_ref, w_ref, bound, m_ref, l_ref, acc, att, part, sums, landed,
    in_sem, w_sem, hop_send, hop_recv, share_send, share_recv, last_send, last_recv,
    sum_send, sum_recv,
):
    ctx, head = lax.axis_index("ctx"), lax.axis_index("head")
    core = lax.rem(ctx, 2)
    other = 1 - core
    rows = q_ref.shape[0]
    heads = q_ref.shape[1] // HEAD_DIM
    half = rows // 2
    width = w_ref.shape[2]
    scale = math.log2(math.e) / math.sqrt(HEAD_DIM)
    after, before = lax.rem(ctx + 2, n_ctx), lax.rem(ctx + n_ctx - 2, n_ctx)
    partner = ctx + 1 - 2 * core
    across = lax.rem(ctx + n_ctx + 2 * core - 1, n_ctx)
    up, down = lax.rem(head + 1, n_head), lax.rem(head + n_head - 1, n_head)

    loads = [
        pltpu.make_async_copy(k_hbm, kv.at[0, core, 0], in_sem.at[0]),
        pltpu.make_async_copy(v_hbm, kv.at[0, core, 1], in_sem.at[1]),
        pltpu.make_async_copy(q_hbm, q_ref, in_sem.at[2]),
    ]
    for load in loads:
        load.start()

    def weight_load(r):
        first = pl.multiple_of(lax.rem(head + r, n_head) * width, width)
        return pltpu.make_async_copy(w_hbm.at[:, pl.ds(first, width)], w_ref.at[r], w_sem.at[r])

    for r in (4, 3, 5, 2, 6, 1, 7, 0):
        weight_load(r).start()

    barrier = pltpu.get_barrier_semaphore()
    for to in (
        (after, head), (before, head), (partner, head), (across, head), (ctx, up), (ctx, down)
    ):
        pl.semaphore_signal(barrier, inc=1, device_id=to, device_id_type=MESH)
    pl.semaphore_wait(barrier, 6)

    def hop(k, piece):
        return pltpu.make_async_remote_copy(
            src_ref=kv.at[k, core, piece],
            dst_ref=kv.at[k + 1, core, piece],
            send_sem=hop_send.at[k, piece],
            recv_sem=hop_recv.at[k, piece],
            device_id=(after, head),
            device_id_type=MESH,
        )

    def share(k, piece):
        return pltpu.make_async_remote_copy(
            src_ref=kv.at[k, core, piece],
            dst_ref=kv.at[k, core, piece],
            send_sem=share_send.at[k, piece],
            recv_sem=share_recv.at[k, piece],
            device_id=(partner, head),
            device_id_type=MESH,
        )

    def last(piece):
        return pltpu.make_async_remote_copy(
            src_ref=kv.at[LAST, 1, piece],
            dst_ref=kv.at[LAST + 1, 1, piece],
            send_sem=last_send.at[piece],
            recv_sem=last_recv.at[piece],
            device_id=(across, head),
            device_id_type=MESH,
        )

    def block(k, parity, first, diagonal=False):
        keys = kv[k, parity, 0]
        values = jnp.transpose(kv[k, parity, 1])
        lowest = bound[0:1, :] - first
        at = lax.broadcasted_iota(jnp.int32, (rows, rows), 0)
        seen = at >= lowest
        if diagonal:
            seen = seen & (at <= lax.broadcasted_iota(jnp.int32, (rows, rows), 1))
        for h in range(heads):
            cols = slice(h * HEAD_DIM, (h + 1) * HEAD_DIM)
            scores = lax.dot_general(
                keys, q_ref[:, cols], (((1,), (1,)), ((), ())), preferred_element_type=jnp.float32
            )
            scores = jnp.where(seen, scores, NEG)
            top = jnp.max(scores, axis=0, keepdims=True)
            if not diagonal:
                old = m_ref[h : h + 1, :]
                top = jnp.maximum(top, old)
            weights = jnp.exp2((scores - top) * scale)
            total = jnp.sum(weights, axis=0, keepdims=True)
            added = jnp.dot(values, weights.astype(jnp.bfloat16), preferred_element_type=jnp.float32)
            if not diagonal:
                fade = jnp.exp2((old - top) * scale)
                total = total + l_ref[h : h + 1, :] * fade
                added = added + acc[cols, :] * fade
            m_ref[h : h + 1, :] = top
            l_ref[h : h + 1, :] = total
            acc[cols, :] = added

    def base(k):
        return (ctx - core - 2 * k) * rows

    for piece in range(2):
        loads[piece].wait()
        hop(0, piece).start()
        share(0, piece).start()

    pos = ctx * rows + lax.broadcasted_iota(jnp.int32, (8, rows), 1)
    start = jnp.zeros((8, rows), jnp.int32)
    for j in range(1, offsets_ref.shape[0] - 1):
        edge = offsets_ref[j]
        start = jnp.maximum(start, jnp.where(pos >= edge, edge, 0))
    bound[...] = start

    loads[2].wait()
    block(0, core, ctx * rows, diagonal=True)

    def stage(k, forward):
        hop(k - 1, 0).wait_recv()
        forward(0)
        share(k, 0).start()
        share(k - 1, 0).wait_recv()
        share(k - 1, 1).wait_recv()
        first = base(k - 1) + other * rows
        block(k - 1, other, jnp.where(first > ctx * rows, UNSEEN, first))
        hop(k - 1, 1).wait_recv()
        forward(1)
        share(k, 1).start()
        block(k, core, base(k) + core * rows)

    def middle(k, carry):
        stage(k, lambda piece: hop(k, piece).start())
        return carry

    lax.fori_loop(1, LAST, middle, 0)

    def tail(piece):
        @pl.when(core == 1)
        def _():
            last(piece).start()

    stage(LAST, tail)
    share(LAST, 0).wait_recv()
    share(LAST, 1).wait_recv()
    block(LAST, other, base(LAST) + other * rows)

    @pl.when(core == 0)
    def _():
        last(0).wait_recv()
        last(1).wait_recv()
        block(LAST + 1, 1, base(LAST + 1) + rows)

    for h in range(heads):
        cols = slice(h * HEAD_DIM, (h + 1) * HEAD_DIM)
        att[:, cols] = jnp.transpose(acc[cols, :] / l_ref[h : h + 1, :]).astype(jnp.bfloat16)

    def send(chain, i):
        return pltpu.make_async_remote_copy(
            src_ref=sums.at[chain, i],
            dst_ref=landed.at[chain, i],
            send_sem=sum_send.at[chain, i],
            recv_sem=sum_recv.at[chain, i],
            device_id=(ctx, up if CHAINS[chain][2] == 1 else down),
            device_id_type=MESH,
        )

    def tokens(chain):
        return slice(CHAINS[chain][3] * half, (CHAINS[chain][3] + 1) * half)

    for r in (4, 5, 3, 6, 2, 7, 1, 0):
        weight_load(r).wait()
        share_of = jnp.dot(att[...], w_ref[r], preferred_element_type=jnp.float32)
        for chain in range(4):
            if stops(chain)[0] == r:
                sums[chain, 0] = share_of[tokens(chain), :].astype(jnp.bfloat16)
        part[r] = share_of
        for chain in range(4):
            if stops(chain)[0] == r:
                send(chain, 0).start()

    for i in range(4):
        for chain in range(4):
            order = stops(chain) + [0]
            if i + 1 >= len(order):
                continue
            send(chain, i).wait_recv()
            mine = part[order[i + 1], tokens(chain), :] + landed[chain, i].astype(jnp.float32)
            if order[i + 1] == 0:
                part[0, tokens(chain), :] = mine
            else:
                sums[chain, i + 1] = mine.astype(jnp.bfloat16)
                send(chain, i + 1).start()
    out_ref[...] = jnp.transpose(part[0]).astype(jnp.bfloat16)

    for chain in range(4):
        for i in range(len(stops(chain))):
            send(chain, i).wait_send()

    def drain(k, carry):
        for piece in range(2):
            share(k, piece).wait_send()

            @pl.when(k < LAST)
            def _():
                hop(k, piece).wait_send()

        return carry

    lax.fori_loop(0, LAST + 1, drain, 0)

    @pl.when(core == 1)
    def _():
        last(0).wait_send()
        last(1).wait_send()


def on_device(n_ctx, n_head, queries, key_vectors, value_vectors, out_weight, offsets):
    rows, columns = queries.shape
    depth, features = out_weight.shape
    width = features // n_head
    dma = pltpu.SemaphoreType.DMA
    return pl.pallas_call(
        functools.partial(kernel, n_ctx, n_head),
        out_shape=jax.ShapeDtypeStruct((width, rows), jnp.bfloat16),
        in_specs=[pl.BlockSpec(memory_space=pltpu.SMEM)] + [pl.BlockSpec(memory_space=pl.ANY)] * 4,
        out_specs=pl.BlockSpec(memory_space=pltpu.VMEM),
        scratch_shapes=[
            pltpu.VMEM((LAST + 2, 2, 2, rows, HEAD_DIM), jnp.bfloat16),
            pltpu.VMEM((rows, columns), jnp.bfloat16),
            pltpu.VMEM((n_head, depth, width), jnp.bfloat16),
            pltpu.VMEM((8, rows), jnp.int32),
            pltpu.VMEM((8, rows), jnp.float32),
            pltpu.VMEM((8, rows), jnp.float32),
            pltpu.VMEM((columns, rows), jnp.float32),
            pltpu.VMEM((rows, columns), jnp.bfloat16),
            pltpu.VMEM((n_head, rows, width), jnp.float32),
            pltpu.VMEM((4, 4, rows // 2, width), jnp.bfloat16),
            pltpu.VMEM((4, 4, rows // 2, width), jnp.bfloat16),
            dma((3,)),
            dma((n_head,)),
            dma((LAST, 2)),
            dma((LAST, 2)),
            dma((LAST + 1, 2)),
            dma((LAST + 1, 2)),
            dma((2,)),
            dma((2,)),
            dma((4, 4)),
            dma((4, 4)),
        ],
        compiler_params=pltpu.CompilerParams(
            collective_id=0, has_side_effects=True, vmem_limit_bytes=40 << 20
        ),
    )(offsets, queries, key_vectors, value_vectors, out_weight)


def solution(mesh):
    placed = (P("ctx", "head"), P("ctx", "head"), P("ctx", "head"), P("head", None), P())
    return jax.shard_map(
        functools.partial(on_device, mesh.shape["ctx"], mesh.shape["head"]),
        mesh=mesh,
        in_specs=placed,
        out_specs=P("head", "ctx"),
        check_vma=False,
    )
```

```python
import functools
import math

import jax
import jax.numpy as jnp
from jax import lax
from jax.experimental import pallas as pl
from jax.experimental.pallas import tpu as pltpu
from jax.sharding import PartitionSpec as P

HEAD_DIM = 128
MESH = pl.DeviceIdType.MESH
NEG = -1e30
FAR = 1 << 24
BARRED = -float(1 << 17)

EDGES = (
    (0, 0, 2), (0, 2, 2), (0, 4, 2), (0, 2, -1), (0, 4, -1), (0, 6, -1), (0, 6, 1),
    (1, 0, 2), (1, 2, 2), (1, 2, -1), (1, 4, -1), (1, 0, 8), (1, 8, -2), (1, 6, 1), (1, 6, -1),
)
SHARED = (range(8), range(9))

CHAINS = ((4, 1, -1, 0), (4, -1, 1, 1), (5, 1, -1, 1), (3, -1, 1, 0))


def stops(chain):
    first, step, _, _ = CHAINS[chain]
    return [r % 8 for r in range(first, 8 if step == 1 else 0, step)]


def kernel(
    n_ctx, n_head, offsets_ref, q_hbm, k_hbm, v_hbm, w_hbm, out_ref,
    kv, q_ref, w_ref, edges, qm, m_ref, acc, att, part, sums, landed,
    in_sem, w_sem, hop_send, hop_recv, share_send, share_recv, last_send, last_recv,
    sum_send, sum_recv,
):
    ctx, head = lax.axis_index("ctx"), lax.axis_index("head")
    core = lax.rem(ctx, 2)
    other = 1 - core
    rows = q_ref.shape[0]
    heads = q_ref.shape[1] // HEAD_DIM
    half = rows // 2
    width = w_ref.shape[2]
    scale = math.log2(math.e) / math.sqrt(HEAD_DIM)
    partner = ctx + 1 - 2 * core
    across = lax.rem(ctx + n_ctx + 6 * core - 3, n_ctx)
    up, down = lax.rem(head + 1, n_head), lax.rem(head + n_head - 1, n_head)

    loads = [
        pltpu.make_async_copy(k_hbm, kv.at[0, core, 0], in_sem.at[0]),
        pltpu.make_async_copy(v_hbm, kv.at[0, core, 1], in_sem.at[1]),
        pltpu.make_async_copy(q_hbm, q_ref, in_sem.at[2]),
    ]
    for load in loads:
        load.start()

    def weight_load(r):
        first = pl.multiple_of(lax.rem(head + r, n_head) * width, width)
        return pltpu.make_async_copy(w_hbm.at[:, pl.ds(first, width)], w_ref.at[r], w_sem.at[r])

    for r in (4, 3, 5, 2, 6, 1, 7, 0):
        weight_load(r).start()

    barrier = pltpu.get_barrier_semaphore()
    for delta in (1, -1, 2, -2, 8, -8):
        near = lax.rem(ctx + n_ctx + 2 * delta, n_ctx)
        pl.semaphore_signal(barrier, inc=1, device_id=(near, head), device_id_type=MESH)
    for to in ((partner, head), (across, head), (ctx, up), (ctx, down)):
        pl.semaphore_signal(barrier, inc=1, device_id=to, device_id_type=MESH)
    pl.semaphore_wait(barrier, 10)

    def chip(delta):
        return lax.rem(ctx + n_ctx + 2 * delta, n_ctx)

    def edge(piece, slot, delta):
        return pltpu.make_async_remote_copy(
            src_ref=kv.at[slot, core, piece],
            dst_ref=kv.at[slot + delta, core, piece],
            send_sem=hop_send.at[piece, slot + delta],
            recv_sem=hop_recv.at[piece, slot + delta],
            device_id=(chip(delta), head),
            device_id_type=MESH,
        )

    def share(piece, slot):
        return pltpu.make_async_remote_copy(
            src_ref=kv.at[slot, core, piece],
            dst_ref=kv.at[slot, core, piece],
            send_sem=share_send.at[piece, slot],
            recv_sem=share_recv.at[piece, slot],
            device_id=(partner, head),
            device_id_type=MESH,
        )

    def last():
        return pltpu.make_async_remote_copy(
            src_ref=kv.at[6, 1, 0],
            dst_ref=kv.at[8, 1, 0],
            send_sem=last_send.at[0],
            recv_sem=last_recv.at[0],
            device_id=(across, head),
            device_id_type=MESH,
        )

    def first_of(slot, parity):
        return (ctx - core - 2 * slot + parity) * rows

    def block(slot, parity, first, diagonal=False):
        keys = kv[slot, parity, 0]
        values = jnp.transpose(kv[slot, parity, 1])
        at = first + lax.broadcasted_iota(jnp.int32, (rows, HEAD_DIM), 0)
        among = (at >= edges[0:1, :]) & (at < edges[8:9, :])
        keys = jnp.concatenate([keys, jnp.where(among, 1.0, 0.0).astype(jnp.bfloat16)], axis=1)
        values = jnp.concatenate([values, jnp.ones((16, rows), jnp.bfloat16)], axis=0)
        if diagonal:
            seen = lax.broadcasted_iota(jnp.int32, (rows, rows), 0) <= lax.broadcasted_iota(
                jnp.int32, (rows, rows), 1
            )

        def score(h):
            got = lax.dot_general(
                keys, qm[h], (((1,), (1,)), ((), ())), preferred_element_type=jnp.float32
            )
            return jnp.where(seen, got, NEG) if diagonal else got

        ready = score(0)
        for h in range(heads):
            scores = ready
            if h + 1 < heads:
                ready = score(h + 1)
            top = jnp.max(scores, axis=0, keepdims=True)
            if not diagonal:
                old = m_ref[h : h + 1, :]
                top = jnp.maximum(top, old)
            weights = jnp.exp2((scores - top) * scale).astype(jnp.bfloat16)
            added = jnp.dot(values, weights, preferred_element_type=jnp.float32)
            if not diagonal:
                added = added + acc[h] * jnp.exp2((old - top) * scale)
            m_ref[h : h + 1, :] = top
            acc[h] = added

    for piece in range(2):
        loads[piece].wait()
        edge(piece, 0, 2).start()
        share(piece, 0).start()
    edge(1, 0, 8).start()

    lane = lax.broadcasted_iota(jnp.int32, (8, HEAD_DIM), 1)
    low = jnp.full((8, HEAD_DIM), FAR, jnp.int32)
    high = low
    n_docs = offsets_ref.shape[0] - 1
    for j in range(n_docs):
        low = jnp.where(lane == j, offsets_ref[j], low)
        high = jnp.where(lane == j, offsets_ref[j + 1], high)
    low = jnp.where(lane == n_docs, -FAR, low)
    high = jnp.where(lane == n_docs, 0, high)
    edges[0:8, :] = low
    edges[8:16, :] = high

    at = ctx * rows + lax.broadcasted_iota(jnp.int32, (rows, HEAD_DIM), 0)
    among = (at >= edges[0:1, :]) & (at < edges[8:9, :])
    barred = jnp.where(among, 0.0, BARRED).astype(jnp.bfloat16)
    loads[2].wait()
    for h in range(heads):
        qm[h, :, 0:HEAD_DIM] = q_ref[:, h * HEAD_DIM : (h + 1) * HEAD_DIM]
        qm[h, :, HEAD_DIM : 2 * HEAD_DIM] = barred

    def mine(slot):
        block(slot, core, first_of(slot, core))

    def theirs(slot):
        share(0, slot).wait_recv()
        share(1, slot).wait_recv()
        block(slot, other, first_of(slot, other))

    def arrived(piece, slot, *deltas):
        edge(piece, slot, 0).wait_recv()
        for delta in deltas:
            edge(piece, slot, delta).start()
        share(piece, slot).start()

    block(0, core, first_of(0, core), diagonal=True)
    share(0, 0).wait_recv()
    share(1, 0).wait_recv()
    block(0, other, jnp.where(core == 0, -FAR // 2, first_of(0, other)))
    arrived(0, 2, 2, -1)
    arrived(1, 2, 2, -1)
    mine(2)
    arrived(1, 8, -2)
    theirs(2)
    arrived(0, 4, 2, -1)
    arrived(1, 4, -1)
    mine(4)
    arrived(0, 1)
    arrived(1, 1)
    mine(1)
    arrived(1, 6, 1, -1)
    theirs(4)
    arrived(0, 6, 1, -1)

    @pl.when(core == 1)
    def _():
        last().start()

    theirs(1)
    mine(6)
    arrived(0, 3)
    arrived(1, 3)
    mine(3)
    theirs(6)
    arrived(0, 5)
    arrived(1, 5)
    theirs(3)
    arrived(0, 7)
    arrived(1, 7)
    mine(5)
    mine(7)
    theirs(5)
    theirs(7)
    share(1, 8).wait_recv()

    @pl.when(core == 0)
    def _():
        last().wait_recv()
        block(8, 1, first_of(8, 1))

    for h in range(heads):
        cols = slice(h * HEAD_DIM, (h + 1) * HEAD_DIM)
        att[:, cols] = jnp.transpose(
            acc[h, 0:HEAD_DIM, :] / acc[h, HEAD_DIM : HEAD_DIM + 1, :]
        ).astype(jnp.bfloat16)

    def send(chain, i):
        return pltpu.make_async_remote_copy(
            src_ref=sums.at[chain, i],
            dst_ref=landed.at[chain, i],
            send_sem=sum_send.at[chain, i],
            recv_sem=sum_recv.at[chain, i],
            device_id=(ctx, up if CHAINS[chain][2] == 1 else down),
            device_id_type=MESH,
        )

    def tokens(chain):
        return slice(CHAINS[chain][3] * half, (CHAINS[chain][3] + 1) * half)

    for r in (4, 5, 3, 6, 2, 7, 1, 0):
        weight_load(r).wait()
        share_of = jnp.dot(att[...], w_ref[r], preferred_element_type=jnp.float32)
        for chain in range(4):
            if stops(chain)[0] == r:
                sums[chain, 0] = share_of[tokens(chain), :].astype(jnp.bfloat16)
        part[r] = share_of
        for chain in range(4):
            if stops(chain)[0] == r:
                send(chain, 0).start()

    for i in range(4):
        for chain in range(4):
            order = stops(chain) + [0]
            if i + 1 >= len(order):
                continue
            send(chain, i).wait_recv()
            mine = part[order[i + 1], tokens(chain), :] + landed[chain, i].astype(jnp.float32)
            if order[i + 1] == 0:
                part[0, tokens(chain), :] = mine
            else:
                sums[chain, i + 1] = mine.astype(jnp.bfloat16)
                send(chain, i + 1).start()
    out_ref[...] = jnp.transpose(part[0]).astype(jnp.bfloat16)

    for chain in range(4):
        for i in range(len(stops(chain))):
            send(chain, i).wait_send()

    for piece, slot, delta in EDGES:
        edge(piece, slot, delta).wait_send()
    for piece in range(2):
        for slot in SHARED[piece]:
            share(piece, slot).wait_send()

    @pl.when(core == 1)
    def _():
        last().wait_send()


def on_device(n_ctx, n_head, queries, key_vectors, value_vectors, out_weight, offsets):
    rows, columns = queries.shape
    depth, features = out_weight.shape
    width = features // n_head
    dma = pltpu.SemaphoreType.DMA
    return pl.pallas_call(
        functools.partial(kernel, n_ctx, n_head),
        out_shape=jax.ShapeDtypeStruct((width, rows), jnp.bfloat16),
        in_specs=[pl.BlockSpec(memory_space=pltpu.SMEM)] + [pl.BlockSpec(memory_space=pl.ANY)] * 4,
        out_specs=pl.BlockSpec(memory_space=pltpu.VMEM),
        scratch_shapes=[
            pltpu.VMEM((9, 2, 2, rows, HEAD_DIM), jnp.bfloat16),
            pltpu.VMEM((rows, columns), jnp.bfloat16),
            pltpu.VMEM((n_head, depth, width), jnp.bfloat16),
            pltpu.VMEM((16, HEAD_DIM), jnp.int32),
            pltpu.VMEM((columns // HEAD_DIM, rows, 2 * HEAD_DIM), jnp.bfloat16),
            pltpu.VMEM((8, rows), jnp.float32),
            pltpu.VMEM((columns // HEAD_DIM, HEAD_DIM + 16, rows), jnp.float32),
            pltpu.VMEM((rows, columns), jnp.bfloat16),
            pltpu.VMEM((n_head, rows, width), jnp.float32),
            pltpu.VMEM((4, 4, rows // 2, width), jnp.bfloat16),
            pltpu.VMEM((4, 4, rows // 2, width), jnp.bfloat16),
            dma((3,)),
            dma((n_head,)),
            dma((2, 9)),
            dma((2, 9)),
            dma((2, 9)),
            dma((2, 9)),
            dma((1,)),
            dma((1,)),
            dma((4, 4)),
            dma((4, 4)),
        ],
        compiler_params=pltpu.CompilerParams(
            collective_id=0, has_side_effects=True, vmem_limit_bytes=60 * 1024 * 1024
        ),
    )(offsets, queries, key_vectors, value_vectors, out_weight)


def solution(mesh):
    placed = (P("ctx", "head"), P("ctx", "head"), P("ctx", "head"), P("head", None), P())
    return jax.shard_map(
        functools.partial(on_device, mesh.shape["ctx"], mesh.shape["head"]),
        mesh=mesh,
        in_specs=placed,
        out_specs=P("head", "ctx"),
        check_vma=False,
    )
```

```python
import functools
import math

import jax
import jax.numpy as jnp
from jax import lax
from jax.experimental import pallas as pl
from jax.experimental.pallas import tpu as pltpu
from jax.sharding import PartitionSpec as P

HEAD_DIM = 128
MESH = pl.DeviceIdType.MESH
NEG = -1e30
FAR = 1 << 24
BARRED = -float(1 << 17)

DEPTH = 12
EDGES = (
    (0, 0, 8, 0xFFF),
    (0, 0, 1, 0xFFF),
    (0, 1, 2, 0xFFF),
    (0, 1, 1, 0xFFF),
    (0, 3, 1, 0xFFF),
    (0, 6, -1, 0xFFF),
    (0, 8, -2, 0xFFF),
    (0, 8, -1, 0xFFF),
    (1, 0, 8, 0xFFF),
    (1, 0, 2, 0xFFF),
    (1, 0, 1, 0xFFF),
    (1, 2, 1, 0xFFF),
    (1, 3, 2, 0xFFF),
    (1, 3, 1, 0xFFF),
    (1, 7, -1, 0xFFF),
    (1, 8, -1, 0xFFF),
)
ORDER = (
    (0, 1), (1, 1), (1, 2), (0, 8), (0, 3), (1, 8), (1, 3), (0, 6),
    (0, 2), (0, 7), (1, 7), (0, 4), (1, 4), (1, 5), (0, 5), (1, 6),
)

CHAINS = ((4, 1, -1, 0), (4, -1, 1, 1), (5, 1, -1, 1), (3, -1, 1, 0))


def stops(chain):
    first, step, _, _ = CHAINS[chain]
    return [r % 8 for r in range(first, 8 if step == 1 else 0, step)]


def kernel(
    n_ctx, n_head, offsets_ref, q_hbm, k_hbm, v_hbm, w_hbm, out_ref,
    kv, q_ref, w_ref, edges, qm, m_ref, acc, att, part, sums, landed,
    in_sem, w_sem, hop_send, hop_recv, share_send, share_recv,
    sum_send, sum_recv,
):
    ctx, head = lax.axis_index("ctx"), lax.axis_index("head")
    core = lax.rem(ctx, 2)
    other = 1 - core
    rows = q_ref.shape[0]
    heads = q_ref.shape[1] // HEAD_DIM
    half = rows // 2
    width = w_ref.shape[2]
    scale = math.log2(math.e) / math.sqrt(HEAD_DIM)
    partner = ctx + 1 - 2 * core
    up, down = lax.rem(head + 1, n_head), lax.rem(head + n_head - 1, n_head)

    loads = [
        pltpu.make_async_copy(k_hbm, kv.at[0, core, 0], in_sem.at[0]),
        pltpu.make_async_copy(v_hbm, kv.at[0, core, 1], in_sem.at[1]),
        pltpu.make_async_copy(q_hbm, q_ref, in_sem.at[2]),
    ]
    for load in loads:
        load.start()

    def weight_load(r):
        first = pl.multiple_of(lax.rem(head + r, n_head) * width, width)
        return pltpu.make_async_copy(w_hbm.at[:, pl.ds(first, width)], w_ref.at[r], w_sem.at[r])

    for r in (4, 3, 5, 2, 6, 1, 7, 0):
        weight_load(r).start()

    barrier = pltpu.get_barrier_semaphore()
    place = lax.rem(lax.div(ctx, 2), DEPTH)

    def holds(mask, at):
        return lax.rem(lax.shift_right_logical(jnp.int32(mask), at), 2)

    def if_sends(mask, act):
        if mask == (1 << DEPTH) - 1:
            act()
        else:
            pl.when(holds(mask, place) == 1)(act)

    reach = {}
    for _, _, delta, mask in EDGES:
        reach[delta] = reach.get(delta, 0) | mask
    count = 3
    for delta, mask in reach.items():
        source = lax.rem(ctx + n_ctx - 2 * delta, n_ctx)
        count = count + holds(mask, place)

        @pl.when(holds(mask, lax.rem(lax.div(source, 2), DEPTH)) == 1)
        def _():
            pl.semaphore_signal(barrier, inc=1, device_id=(source, head), device_id_type=MESH)

    for to in ((partner, head), (ctx, up), (ctx, down)):
        pl.semaphore_signal(barrier, inc=1, device_id=to, device_id_type=MESH)
    pl.semaphore_wait(barrier, count)

    def chip(delta):
        return lax.rem(ctx + n_ctx + 2 * delta, n_ctx)

    def edge(piece, slot, delta):
        return pltpu.make_async_remote_copy(
            src_ref=kv.at[slot, core, piece],
            dst_ref=kv.at[slot + delta, core, piece],
            send_sem=hop_send.at[piece, slot, slot + delta],
            recv_sem=hop_recv.at[piece, slot + delta],
            device_id=(chip(delta), head),
            device_id_type=MESH,
        )

    def share(piece, slot):
        return pltpu.make_async_remote_copy(
            src_ref=kv.at[slot, core, piece],
            dst_ref=kv.at[slot, core, piece],
            send_sem=share_send.at[piece, slot],
            recv_sem=share_recv.at[piece, slot],
            device_id=(partner, head),
            device_id_type=MESH,
        )

    def pass_on(piece, slot):
        for kind, at, delta, mask in EDGES:
            if (kind, at) == (piece, slot):
                if_sends(mask, lambda: edge(piece, slot, delta).start())
        share(piece, slot).start()

    def first_of(slot, parity):
        return (ctx - core - 2 * slot + parity) * rows

    def block(slot, parity, first, diagonal=False):
        keys = kv[slot, parity, 0]
        values = jnp.transpose(kv[slot, parity, 1])
        at = first + lax.broadcasted_iota(jnp.int32, (rows, HEAD_DIM), 0)
        among = (at >= edges[0:1, :]) & (at < edges[8:9, :])
        keys = jnp.concatenate([keys, jnp.where(among, 1.0, 0.0).astype(jnp.bfloat16)], axis=1)
        values = jnp.concatenate([values, jnp.ones((16, rows), jnp.bfloat16)], axis=0)
        if diagonal:
            seen = lax.broadcasted_iota(jnp.int32, (rows, rows), 0) <= lax.broadcasted_iota(
                jnp.int32, (rows, rows), 1
            )

        def score(h):
            got = lax.dot_general(
                keys, qm[h], (((1,), (1,)), ((), ())), preferred_element_type=jnp.float32
            )
            return jnp.where(seen, got, NEG) if diagonal else got

        ready = score(0)
        for h in range(heads):
            scores = ready
            if h + 1 < heads:
                ready = score(h + 1)
            top = jnp.max(scores, axis=0, keepdims=True)
            if not diagonal:
                old = m_ref[h : h + 1, :]
                top = jnp.maximum(top, old)
            weights = jnp.exp2((scores - top) * scale).astype(jnp.bfloat16)
            added = jnp.dot(values, weights, preferred_element_type=jnp.float32)
            if not diagonal:
                added = added + acc[h] * jnp.exp2((old - top) * scale)
            m_ref[h : h + 1, :] = top
            acc[h] = added

    for piece in range(2):
        loads[piece].wait()
        pass_on(piece, 0)

    lane = lax.broadcasted_iota(jnp.int32, (8, HEAD_DIM), 1)
    low = jnp.full((8, HEAD_DIM), FAR, jnp.int32)
    high = low
    n_docs = offsets_ref.shape[0] - 1
    for j in range(n_docs):
        low = jnp.where(lane == j, offsets_ref[j], low)
        high = jnp.where(lane == j, offsets_ref[j + 1], high)
    low = jnp.where(lane == n_docs, -FAR, low)
    high = jnp.where(lane == n_docs, 0, high)
    edges[0:8, :] = low
    edges[8:16, :] = high

    at = ctx * rows + lax.broadcasted_iota(jnp.int32, (rows, HEAD_DIM), 0)
    among = (at >= edges[0:1, :]) & (at < edges[8:9, :])
    barred = jnp.where(among, 0.0, BARRED).astype(jnp.bfloat16)
    loads[2].wait()
    for h in range(heads):
        qm[h, :, 0:HEAD_DIM] = q_ref[:, h * HEAD_DIM : (h + 1) * HEAD_DIM]
        qm[h, :, HEAD_DIM : 2 * HEAD_DIM] = barred

    def mine(slot):
        block(slot, core, first_of(slot, core))

    def theirs(slot):
        share(0, slot).wait_recv()
        share(1, slot).wait_recv()
        block(slot, other, first_of(slot, other))

    def oldest():
        share(0, 8).wait_recv()
        share(1, 8).wait_recv()

        @pl.when(core == 0)
        def _():
            block(8, 1, first_of(8, 1))

    def first_theirs():
        share(0, 0).wait_recv()
        share(1, 0).wait_recv()
        block(0, other, jnp.where(core == 0, -FAR // 2, first_of(0, other)))

    block(0, core, first_of(0, core), diagonal=True)
    due = [first_theirs]
    here = set()
    for piece, slot in ORDER:
        edge(piece, slot, 0).wait_recv()
        pass_on(piece, slot)
        if slot in here:
            if due:
                due.pop(0)()
            if slot == 8:
                due.append(oldest)
            else:
                mine(slot)
                due.append(functools.partial(theirs, slot))
        here.add(slot)
    for left in due:
        left()

    for h in range(heads):
        cols = slice(h * HEAD_DIM, (h + 1) * HEAD_DIM)
        att[:, cols] = jnp.transpose(
            acc[h, 0:HEAD_DIM, :] / acc[h, HEAD_DIM : HEAD_DIM + 1, :]
        ).astype(jnp.bfloat16)

    def send(chain, i):
        return pltpu.make_async_remote_copy(
            src_ref=sums.at[chain, i],
            dst_ref=landed.at[chain, i],
            send_sem=sum_send.at[chain, i],
            recv_sem=sum_recv.at[chain, i],
            device_id=(ctx, up if CHAINS[chain][2] == 1 else down),
            device_id_type=MESH,
        )

    def tokens(chain):
        return slice(CHAINS[chain][3] * half, (CHAINS[chain][3] + 1) * half)

    for r in (4, 5, 3, 6, 2, 7, 1, 0):
        weight_load(r).wait()
        share_of = jnp.dot(att[...], w_ref[r], preferred_element_type=jnp.float32)
        for chain in range(4):
            if stops(chain)[0] == r:
                sums[chain, 0] = share_of[tokens(chain), :].astype(jnp.bfloat16)
        part[r] = share_of
        for chain in range(4):
            if stops(chain)[0] == r:
                send(chain, 0).start()

    for i in range(4):
        for chain in range(4):
            order = stops(chain) + [0]
            if i + 1 >= len(order):
                continue
            send(chain, i).wait_recv()
            mine = part[order[i + 1], tokens(chain), :] + landed[chain, i].astype(jnp.float32)
            if order[i + 1] == 0:
                part[0, tokens(chain), :] = mine
            else:
                sums[chain, i + 1] = mine.astype(jnp.bfloat16)
                send(chain, i + 1).start()
    out_ref[...] = jnp.transpose(part[0]).astype(jnp.bfloat16)

    for chain in range(4):
        for i in range(len(stops(chain))):
            send(chain, i).wait_send()

    for piece, at, delta, mask in EDGES:
        if_sends(mask, lambda: edge(piece, at, delta).wait_send())
    for piece in range(2):
        for slot in range(9):
            share(piece, slot).wait_send()


def on_device(n_ctx, n_head, queries, key_vectors, value_vectors, out_weight, offsets):
    rows, columns = queries.shape
    depth, features = out_weight.shape
    width = features // n_head
    dma = pltpu.SemaphoreType.DMA
    return pl.pallas_call(
        functools.partial(kernel, n_ctx, n_head),
        out_shape=jax.ShapeDtypeStruct((width, rows), jnp.bfloat16),
        in_specs=[pl.BlockSpec(memory_space=pltpu.SMEM)] + [pl.BlockSpec(memory_space=pl.ANY)] * 4,
        out_specs=pl.BlockSpec(memory_space=pltpu.VMEM),
        scratch_shapes=[
            pltpu.VMEM((9, 2, 2, rows, HEAD_DIM), jnp.bfloat16),
            pltpu.VMEM((rows, columns), jnp.bfloat16),
            pltpu.VMEM((n_head, depth, width), jnp.bfloat16),
            pltpu.VMEM((16, HEAD_DIM), jnp.int32),
            pltpu.VMEM((columns // HEAD_DIM, rows, 2 * HEAD_DIM), jnp.bfloat16),
            pltpu.VMEM((8, rows), jnp.float32),
            pltpu.VMEM((columns // HEAD_DIM, HEAD_DIM + 16, rows), jnp.float32),
            pltpu.VMEM((rows, columns), jnp.bfloat16),
            pltpu.VMEM((n_head, rows, width), jnp.float32),
            pltpu.VMEM((4, 4, rows // 2, width), jnp.bfloat16),
            pltpu.VMEM((4, 4, rows // 2, width), jnp.bfloat16),
            dma((3,)),
            dma((n_head,)),
            dma((2, 9, 9)),
            dma((2, 9)),
            dma((2, 9)),
            dma((2, 9)),
            dma((4, 4)),
            dma((4, 4)),
        ],
        compiler_params=pltpu.CompilerParams(
            collective_id=0, has_side_effects=True, vmem_limit_bytes=60 * 1024 * 1024
        ),
    )(offsets, queries, key_vectors, value_vectors, out_weight)


def solution(mesh):
    placed = (P("ctx", "head"), P("ctx", "head"), P("ctx", "head"), P("head", None), P())
    return jax.shard_map(
        functools.partial(on_device, mesh.shape["ctx"], mesh.shape["head"]),
        mesh=mesh,
        in_specs=placed,
        out_specs=P("head", "ctx"),
        check_vma=False,
    )
```

```python
import functools
import math

import jax
import jax.numpy as jnp
from jax import lax
from jax.experimental import pallas as pl
from jax.experimental.pallas import tpu as pltpu
from jax.sharding import PartitionSpec as P

HEAD_DIM = 128
MESH = pl.DeviceIdType.MESH
NEG = -1e30
FAR = 1 << 24
BARRED = -float(1 << 17)

DEPTH = 12
EDGES = (
    (0, 0, 8, 0xFFF),
    (0, 0, 1, 0xFFF),
    (0, 1, 2, 0xFFF),
    (0, 1, 1, 0xFFF),
    (0, 3, 1, 0xFFF),
    (0, 6, -1, 0xFFF),
    (0, 8, -2, 0xFFF),
    (0, 8, -1, 0xFFF),
    (1, 0, 8, 0xFFF),
    (1, 0, 2, 0xFFF),
    (1, 0, 1, 0xFFF),
    (1, 2, 1, 0xFFF),
    (1, 3, 2, 0xFFF),
    (1, 3, 1, 0xFFF),
    (1, 7, -1, 0xFFF),
    (1, 8, -1, 0xFFF),
)
ORDER = (
    (0, 1), (1, 1), (1, 2), (0, 8), (0, 3), (1, 8), (1, 3), (0, 6),
    (0, 2), (0, 7), (1, 7), (0, 4), (1, 4), (1, 5), (0, 5), (1, 6),
)

CHAINS = ((4, 1, -1, 0), (4, -1, 1, 1), (5, 1, -1, 1), (3, -1, 1, 0))


def stops(chain):
    first, step, _, _ = CHAINS[chain]
    return [r % 8 for r in range(first, 8 if step == 1 else 0, step)]


def kernel(
    n_ctx, n_head, offsets_ref, q_hbm, k_hbm, v_hbm, w_hbm, out_ref,
    kv, q_ref, w_ref, edges, qm, m_ref, acc, att, part, sums, landed,
    in_sem, w_sem, hop_send, hop_recv, share_send, share_recv,
    sum_send, sum_recv,
):
    ctx, head = lax.axis_index("ctx"), lax.axis_index("head")
    core = lax.rem(ctx, 2)
    other = 1 - core
    rows = q_ref.shape[0]
    heads = q_ref.shape[1] // HEAD_DIM
    half = rows // 2
    width = w_ref.shape[2]
    scale = math.log2(math.e) / math.sqrt(HEAD_DIM)
    partner = ctx + 1 - 2 * core
    up, down = lax.rem(head + 1, n_head), lax.rem(head + n_head - 1, n_head)

    loads = [
        pltpu.make_async_copy(k_hbm, kv.at[0, core, 0], in_sem.at[0]),
        pltpu.make_async_copy(v_hbm, kv.at[0, core, 1], in_sem.at[1]),
        pltpu.make_async_copy(q_hbm, q_ref, in_sem.at[2]),
    ]
    for load in loads:
        load.start()

    def weight_load(r):
        first = pl.multiple_of(lax.rem(head + r, n_head) * width, width)
        return pltpu.make_async_copy(w_hbm.at[:, pl.ds(first, width)], w_ref.at[r], w_sem.at[r])

    for r in (4, 3, 5, 2, 6, 1, 7, 0):
        weight_load(r).start()

    barrier = pltpu.get_barrier_semaphore()
    place = lax.rem(lax.div(ctx, 2), DEPTH)

    def holds(mask, at):
        return lax.rem(lax.shift_right_logical(jnp.int32(mask), at), 2)

    def if_sends(mask, act):
        if mask == (1 << DEPTH) - 1:
            act()
        else:
            pl.when(holds(mask, place) == 1)(act)

    reach = {}
    for _, _, delta, mask in EDGES:
        reach[delta] = reach.get(delta, 0) | mask
    count = 3
    for delta, mask in reach.items():
        source = lax.rem(ctx + n_ctx - 2 * delta, n_ctx)
        count = count + holds(mask, place)

        @pl.when(holds(mask, lax.rem(lax.div(source, 2), DEPTH)) == 1)
        def _():
            pl.semaphore_signal(barrier, inc=1, device_id=(source, head), device_id_type=MESH)

    for to in ((partner, head), (ctx, up), (ctx, down)):
        pl.semaphore_signal(barrier, inc=1, device_id=to, device_id_type=MESH)
    pl.semaphore_wait(barrier, count)

    def chip(delta):
        return lax.rem(ctx + n_ctx + 2 * delta, n_ctx)

    def edge(piece, slot, delta):
        return pltpu.make_async_remote_copy(
            src_ref=kv.at[slot, core, piece],
            dst_ref=kv.at[slot + delta, core, piece],
            send_sem=hop_send.at[piece, slot, slot + delta],
            recv_sem=hop_recv.at[piece, slot + delta],
            device_id=(chip(delta), head),
            device_id_type=MESH,
        )

    def share(piece, slot):
        return pltpu.make_async_remote_copy(
            src_ref=kv.at[slot, core, piece],
            dst_ref=kv.at[slot, core, piece],
            send_sem=share_send.at[piece, slot],
            recv_sem=share_recv.at[piece, slot],
            device_id=(partner, head),
            device_id_type=MESH,
        )

    def pass_on(piece, slot):
        for kind, at, delta, mask in EDGES:
            if (kind, at) == (piece, slot):
                if_sends(mask, lambda: edge(piece, slot, delta).start())
        share(piece, slot).start()

    def first_of(slot, parity):
        return (ctx - core - 2 * slot + parity) * rows

    def blocks(group, diagonal=False):
        keys, values = [], []
        for slot, parity, first in group:
            at = first + lax.broadcasted_iota(jnp.int32, (rows, HEAD_DIM), 0)
            among = (at >= edges[0:1, :]) & (at < edges[8:9, :])
            named = jnp.where(among, 1.0, 0.0).astype(jnp.bfloat16)
            keys.append(jnp.concatenate([kv[slot, parity, 0], named], axis=1))
            values.append(jnp.transpose(kv[slot, parity, 1]))
        keys = jnp.concatenate(keys, axis=0)
        values = jnp.concatenate(values, axis=1)
        values = jnp.concatenate([values, jnp.ones((16, keys.shape[0]), jnp.bfloat16)], axis=0)
        if diagonal:
            key_at = lax.broadcasted_iota(jnp.int32, (keys.shape[0], rows), 0)
            query_at = lax.broadcasted_iota(jnp.int32, (keys.shape[0], rows), 1)
            seen = (key_at >= rows) | (key_at <= query_at)

        def score(h):
            got = lax.dot_general(
                keys, qm[h], (((1,), (1,)), ((), ())), preferred_element_type=jnp.float32
            )
            return jnp.where(seen, got, NEG) if diagonal else got

        ready = score(0)
        for h in range(heads):
            scores = ready
            if h + 1 < heads:
                ready = score(h + 1)
            top = jnp.max(scores, axis=0, keepdims=True)
            if not diagonal:
                old = m_ref[h : h + 1, :]
                top = jnp.maximum(top, old)
            weights = jnp.exp2((scores - top) * scale).astype(jnp.bfloat16)
            added = jnp.dot(values, weights, preferred_element_type=jnp.float32)
            if not diagonal:
                added = added + acc[h] * jnp.exp2((old - top) * scale)
            m_ref[h : h + 1, :] = top
            acc[h] = added

    for piece in range(2):
        loads[piece].wait()
        pass_on(piece, 0)

    lane = lax.broadcasted_iota(jnp.int32, (8, HEAD_DIM), 1)
    low = jnp.full((8, HEAD_DIM), FAR, jnp.int32)
    high = low
    n_docs = offsets_ref.shape[0] - 1
    for j in range(n_docs):
        low = jnp.where(lane == j, offsets_ref[j], low)
        high = jnp.where(lane == j, offsets_ref[j + 1], high)
    low = jnp.where(lane == n_docs, -FAR, low)
    high = jnp.where(lane == n_docs, 0, high)
    edges[0:8, :] = low
    edges[8:16, :] = high

    at = ctx * rows + lax.broadcasted_iota(jnp.int32, (rows, HEAD_DIM), 0)
    among = (at >= edges[0:1, :]) & (at < edges[8:9, :])
    barred = jnp.where(among, 0.0, BARRED).astype(jnp.bfloat16)
    loads[2].wait()
    for h in range(heads):
        qm[h, :, 0:HEAD_DIM] = q_ref[:, h * HEAD_DIM : (h + 1) * HEAD_DIM]
        qm[h, :, HEAD_DIM : 2 * HEAD_DIM] = barred

    def shared(slot):
        share(0, slot).wait_recv()
        share(1, slot).wait_recv()

    def theirs(slot):
        shared(slot)
        return (slot, other, first_of(slot, other))

    blocks([(0, core, first_of(0, core))], diagonal=True)
    shared(0)
    due = [(0, other, jnp.where(core == 0, -FAR // 2, first_of(0, other)))]
    waiting = []
    here = set()
    for piece, slot in ORDER:
        edge(piece, slot, 0).wait_recv()
        pass_on(piece, slot)
        if slot in here and slot != 8:
            if not due:
                due.append(theirs(waiting.pop(0)))
            blocks([due.pop(0), (slot, core, first_of(slot, core))])
            waiting.append(slot)
        here.add(slot)
    while waiting:
        due.append(theirs(waiting.pop(0)))
        if len(due) == 2 or not waiting:
            blocks(due)
            due = []
    shared(8)

    @pl.when(core == 0)
    def _():
        blocks([(8, 1, first_of(8, 1))])

    for h in range(heads):
        cols = slice(h * HEAD_DIM, (h + 1) * HEAD_DIM)
        att[:, cols] = jnp.transpose(
            acc[h, 0:HEAD_DIM, :] / acc[h, HEAD_DIM : HEAD_DIM + 1, :]
        ).astype(jnp.bfloat16)

    def send(chain, i):
        return pltpu.make_async_remote_copy(
            src_ref=sums.at[chain, i],
            dst_ref=landed.at[chain, i],
            send_sem=sum_send.at[chain, i],
            recv_sem=sum_recv.at[chain, i],
            device_id=(ctx, up if CHAINS[chain][2] == 1 else down),
            device_id_type=MESH,
        )

    def tokens(chain):
        return slice(CHAINS[chain][3] * half, (CHAINS[chain][3] + 1) * half)

    for r in (4, 5, 3, 6, 2, 7, 1, 0):
        weight_load(r).wait()
        share_of = jnp.dot(att[...], w_ref[r], preferred_element_type=jnp.float32)
        for chain in range(4):
            if stops(chain)[0] == r:
                sums[chain, 0] = share_of[tokens(chain), :].astype(jnp.bfloat16)
        part[r] = share_of
        for chain in range(4):
            if stops(chain)[0] == r:
                send(chain, 0).start()

    for i in range(4):
        for chain in range(4):
            order = stops(chain) + [0]
            if i + 1 >= len(order):
                continue
            send(chain, i).wait_recv()
            mine = part[order[i + 1], tokens(chain), :] + landed[chain, i].astype(jnp.float32)
            if order[i + 1] == 0:
                part[0, tokens(chain), :] = mine
            else:
                sums[chain, i + 1] = mine.astype(jnp.bfloat16)
                send(chain, i + 1).start()
    out_ref[...] = jnp.transpose(part[0]).astype(jnp.bfloat16)

    for chain in range(4):
        for i in range(len(stops(chain))):
            send(chain, i).wait_send()

    for piece, at, delta, mask in EDGES:
        if_sends(mask, lambda: edge(piece, at, delta).wait_send())
    for piece in range(2):
        for slot in range(9):
            share(piece, slot).wait_send()


def on_device(n_ctx, n_head, queries, key_vectors, value_vectors, out_weight, offsets):
    rows, columns = queries.shape
    depth, features = out_weight.shape
    width = features // n_head
    dma = pltpu.SemaphoreType.DMA
    return pl.pallas_call(
        functools.partial(kernel, n_ctx, n_head),
        out_shape=jax.ShapeDtypeStruct((width, rows), jnp.bfloat16),
        in_specs=[pl.BlockSpec(memory_space=pltpu.SMEM)] + [pl.BlockSpec(memory_space=pl.ANY)] * 4,
        out_specs=pl.BlockSpec(memory_space=pltpu.VMEM),
        scratch_shapes=[
            pltpu.VMEM((9, 2, 2, rows, HEAD_DIM), jnp.bfloat16),
            pltpu.VMEM((rows, columns), jnp.bfloat16),
            pltpu.VMEM((n_head, depth, width), jnp.bfloat16),
            pltpu.VMEM((16, HEAD_DIM), jnp.int32),
            pltpu.VMEM((columns // HEAD_DIM, rows, 2 * HEAD_DIM), jnp.bfloat16),
            pltpu.VMEM((8, rows), jnp.float32),
            pltpu.VMEM((columns // HEAD_DIM, HEAD_DIM + 16, rows), jnp.float32),
            pltpu.VMEM((rows, columns), jnp.bfloat16),
            pltpu.VMEM((n_head, rows, width), jnp.float32),
            pltpu.VMEM((4, 4, rows // 2, width), jnp.bfloat16),
            pltpu.VMEM((4, 4, rows // 2, width), jnp.bfloat16),
            dma((3,)),
            dma((n_head,)),
            dma((2, 9, 9)),
            dma((2, 9)),
            dma((2, 9)),
            dma((2, 9)),
            dma((4, 4)),
            dma((4, 4)),
        ],
        compiler_params=pltpu.CompilerParams(
            collective_id=0, has_side_effects=True, vmem_limit_bytes=60 * 1024 * 1024
        ),
    )(offsets, queries, key_vectors, value_vectors, out_weight)


def solution(mesh):
    placed = (P("ctx", "head"), P("ctx", "head"), P("ctx", "head"), P("head", None), P())
    return jax.shard_map(
        functools.partial(on_device, mesh.shape["ctx"], mesh.shape["head"]),
        mesh=mesh,
        in_specs=placed,
        out_specs=P("head", "ctx"),
        check_vma=False,
    )
```

```python
import functools
import math

import jax
import jax.numpy as jnp
from jax import lax
from jax.experimental import pallas as pl
from jax.experimental.pallas import tpu as pltpu
from jax.sharding import PartitionSpec as P

HEAD_DIM = 128
MESH = pl.DeviceIdType.MESH
NEG = -1e30
FAR = 1 << 24
BARRED = -float(1 << 17)

DEPTH = 12
EDGES = (
    (0, 0, 8, 0xFFF),
    (0, 0, 1, 0xFFF),
    (0, 1, 2, 0xFFF),
    (0, 1, 1, 0xFFF),
    (0, 3, 1, 0xFFF),
    (0, 6, -1, 0xFFF),
    (0, 8, -2, 0xFFF),
    (0, 8, -1, 0xFFF),
    (1, 0, 8, 0xFFF),
    (1, 0, 2, 0xFFF),
    (1, 0, 1, 0xFFF),
    (1, 2, 1, 0xFFF),
    (1, 3, 2, 0xFFF),
    (1, 3, 1, 0xFFF),
    (1, 7, -1, 0xFFF),
    (1, 8, -1, 0xFFF),
)
ORDER = (
    (0, 1), (1, 1), (1, 2), (0, 8), (0, 3), (1, 8), (1, 3), (0, 6),
    (0, 2), (0, 7), (1, 7), (0, 4), (1, 4), (1, 5), (0, 5), (1, 6),
)

CHAINS = (
    (4, 1, -1, 0), (4, -1, 1, 2), (4, 1, -1, 1), (4, -1, 1, 3),
    (5, 1, -1, 2), (3, -1, 1, 0), (5, 1, -1, 3), (3, -1, 1, 1),
)


def stops(chain):
    first, step, _, _ = CHAINS[chain]
    return [r % 8 for r in range(first, 8 if step == 1 else 0, step)]


def kernel(
    n_ctx, n_head, offsets_ref, q_hbm, k_hbm, v_hbm, w_hbm, out_ref,
    kv, q_ref, w_ref, edges, qm, m_ref, acc, att, part, sums, landed,
    in_sem, w_sem, hop_send, hop_recv, share_send, share_recv,
    sum_send, sum_recv,
):
    ctx, head = lax.axis_index("ctx"), lax.axis_index("head")
    core = lax.rem(ctx, 2)
    other = 1 - core
    rows = q_ref.shape[0]
    heads = q_ref.shape[1] // HEAD_DIM
    part_rows = rows // 4
    width = w_ref.shape[2]
    scale = math.log2(math.e) / math.sqrt(HEAD_DIM)
    partner = ctx + 1 - 2 * core
    up, down = lax.rem(head + 1, n_head), lax.rem(head + n_head - 1, n_head)

    loads = [
        pltpu.make_async_copy(k_hbm, kv.at[0, core, 0], in_sem.at[0]),
        pltpu.make_async_copy(v_hbm, kv.at[0, core, 1], in_sem.at[1]),
        pltpu.make_async_copy(q_hbm, q_ref, in_sem.at[2]),
    ]
    for load in loads:
        load.start()

    def weight_load(r):
        first = pl.multiple_of(lax.rem(head + r, n_head) * width, width)
        return pltpu.make_async_copy(w_hbm.at[:, pl.ds(first, width)], w_ref.at[r], w_sem.at[r])

    for r in (4, 3, 5, 2, 6, 1, 7, 0):
        weight_load(r).start()

    barrier = pltpu.get_barrier_semaphore()
    place = lax.rem(lax.div(ctx, 2), DEPTH)

    def holds(mask, at):
        return lax.rem(lax.shift_right_logical(jnp.int32(mask), at), 2)

    def if_sends(mask, act):
        if mask == (1 << DEPTH) - 1:
            act()
        else:
            pl.when(holds(mask, place) == 1)(act)

    reach = {}
    for _, _, delta, mask in EDGES:
        reach[delta] = reach.get(delta, 0) | mask
    count = 3
    for delta, mask in reach.items():
        source = lax.rem(ctx + n_ctx - 2 * delta, n_ctx)
        count = count + holds(mask, place)

        @pl.when(holds(mask, lax.rem(lax.div(source, 2), DEPTH)) == 1)
        def _():
            pl.semaphore_signal(barrier, inc=1, device_id=(source, head), device_id_type=MESH)

    for to in ((partner, head), (ctx, up), (ctx, down)):
        pl.semaphore_signal(barrier, inc=1, device_id=to, device_id_type=MESH)
    pl.semaphore_wait(barrier, count)

    def chip(delta):
        return lax.rem(ctx + n_ctx + 2 * delta, n_ctx)

    def edge(piece, slot, delta):
        return pltpu.make_async_remote_copy(
            src_ref=kv.at[slot, core, piece],
            dst_ref=kv.at[slot + delta, core, piece],
            send_sem=hop_send.at[piece, slot, slot + delta],
            recv_sem=hop_recv.at[piece, slot + delta],
            device_id=(chip(delta), head),
            device_id_type=MESH,
        )

    def share(piece, slot):
        return pltpu.make_async_remote_copy(
            src_ref=kv.at[slot, core, piece],
            dst_ref=kv.at[slot, core, piece],
            send_sem=share_send.at[piece, slot],
            recv_sem=share_recv.at[piece, slot],
            device_id=(partner, head),
            device_id_type=MESH,
        )

    def pass_on(piece, slot):
        for kind, at, delta, mask in EDGES:
            if (kind, at) == (piece, slot):
                if_sends(mask, lambda: edge(piece, slot, delta).start())
        share(piece, slot).start()

    def first_of(slot, parity):
        return (ctx - core - 2 * slot + parity) * rows

    def blocks(group, diagonal=False):
        keys, values = [], []
        for slot, parity, first in group:
            at = first + lax.broadcasted_iota(jnp.int32, (rows, HEAD_DIM), 0)
            among = (at >= edges[0:1, :]) & (at < edges[8:9, :])
            named = jnp.where(among, 1.0, 0.0).astype(jnp.bfloat16)
            keys.append(jnp.concatenate([kv[slot, parity, 0], named], axis=1))
            values.append(jnp.transpose(kv[slot, parity, 1]))
        keys = jnp.concatenate(keys, axis=0)
        values = jnp.concatenate(values, axis=1)
        values = jnp.concatenate([values, jnp.ones((16, keys.shape[0]), jnp.bfloat16)], axis=0)
        if diagonal:
            key_at = lax.broadcasted_iota(jnp.int32, (keys.shape[0], rows), 0)
            query_at = lax.broadcasted_iota(jnp.int32, (keys.shape[0], rows), 1)
            seen = (key_at >= rows) | (key_at <= query_at)

        def score(h):
            got = lax.dot_general(
                keys, qm[h], (((1,), (1,)), ((), ())), preferred_element_type=jnp.float32
            )
            return jnp.where(seen, got, NEG) if diagonal else got

        ready = score(0)
        for h in range(heads):
            scores = ready
            if h + 1 < heads:
                ready = score(h + 1)
            top = jnp.max(scores, axis=0, keepdims=True)
            if not diagonal:
                old = m_ref[h : h + 1, :]
                top = jnp.maximum(top, old)
            weights = jnp.exp2((scores - top) * scale).astype(jnp.bfloat16)
            added = jnp.dot(values, weights, preferred_element_type=jnp.float32)
            if not diagonal:
                added = added + acc[h] * jnp.exp2((old - top) * scale)
            m_ref[h : h + 1, :] = top
            acc[h] = added

    for piece in range(2):
        loads[piece].wait()
        pass_on(piece, 0)

    lane = lax.broadcasted_iota(jnp.int32, (8, HEAD_DIM), 1)
    low = jnp.full((8, HEAD_DIM), FAR, jnp.int32)
    high = low
    n_docs = offsets_ref.shape[0] - 1
    for j in range(n_docs):
        low = jnp.where(lane == j, offsets_ref[j], low)
        high = jnp.where(lane == j, offsets_ref[j + 1], high)
    low = jnp.where(lane == n_docs, -FAR, low)
    high = jnp.where(lane == n_docs, 0, high)
    edges[0:8, :] = low
    edges[8:16, :] = high

    at = ctx * rows + lax.broadcasted_iota(jnp.int32, (rows, HEAD_DIM), 0)
    among = (at >= edges[0:1, :]) & (at < edges[8:9, :])
    barred = jnp.where(among, 0.0, BARRED).astype(jnp.bfloat16)
    loads[2].wait()
    for h in range(heads):
        qm[h, :, 0:HEAD_DIM] = q_ref[:, h * HEAD_DIM : (h + 1) * HEAD_DIM]
        qm[h, :, HEAD_DIM : 2 * HEAD_DIM] = barred

    def shared(slot):
        share(0, slot).wait_recv()
        share(1, slot).wait_recv()

    def theirs(slot):
        shared(slot)
        return (slot, other, first_of(slot, other))

    blocks([(0, core, first_of(0, core))], diagonal=True)
    shared(0)
    due = [(0, other, jnp.where(core == 0, -FAR // 2, first_of(0, other)))]
    waiting = []
    here = set()
    for piece, slot in ORDER:
        edge(piece, slot, 0).wait_recv()
        pass_on(piece, slot)
        if slot in here and slot != 8:
            if not due:
                due.append(theirs(waiting.pop(0)))
            blocks([due.pop(0), (slot, core, first_of(slot, core))])
            waiting.append(slot)
        here.add(slot)
    while waiting:
        due.append(theirs(waiting.pop(0)))
        if len(due) == 2 or not waiting:
            blocks(due)
            due = []
    shared(8)

    @pl.when(core == 0)
    def _():
        blocks([(8, 1, first_of(8, 1))])

    for h in range(heads):
        cols = slice(h * HEAD_DIM, (h + 1) * HEAD_DIM)
        att[:, cols] = jnp.transpose(
            acc[h, 0:HEAD_DIM, :] / acc[h, HEAD_DIM : HEAD_DIM + 1, :]
        ).astype(jnp.bfloat16)

    def send(chain, i):
        return pltpu.make_async_remote_copy(
            src_ref=sums.at[chain, i],
            dst_ref=landed.at[chain, i],
            send_sem=sum_send.at[chain, i],
            recv_sem=sum_recv.at[chain, i],
            device_id=(ctx, up if CHAINS[chain][2] == 1 else down),
            device_id_type=MESH,
        )

    def tokens(chain):
        return slice(CHAINS[chain][3] * part_rows, (CHAINS[chain][3] + 1) * part_rows)

    for r in (4, 5, 3, 6, 2, 7, 1, 0):
        weight_load(r).wait()
        share_of = jnp.dot(att[...], w_ref[r], preferred_element_type=jnp.float32)
        for chain in range(len(CHAINS)):
            if stops(chain)[0] == r:
                sums[chain, 0] = share_of[tokens(chain), :].astype(jnp.bfloat16)
        part[r] = share_of
        for chain in range(len(CHAINS)):
            if stops(chain)[0] == r:
                send(chain, 0).start()

    for i in range(4):
        for chain in range(len(CHAINS)):
            order = stops(chain) + [0]
            if i + 1 >= len(order):
                continue
            send(chain, i).wait_recv()
            mine = part[order[i + 1], tokens(chain), :] + landed[chain, i].astype(jnp.float32)
            if order[i + 1] == 0:
                part[0, tokens(chain), :] = mine
            else:
                sums[chain, i + 1] = mine.astype(jnp.bfloat16)
                send(chain, i + 1).start()
    out_ref[...] = jnp.transpose(part[0]).astype(jnp.bfloat16)

    for chain in range(len(CHAINS)):
        for i in range(len(stops(chain))):
            send(chain, i).wait_send()

    for piece, at, delta, mask in EDGES:
        if_sends(mask, lambda: edge(piece, at, delta).wait_send())
    for piece in range(2):
        for slot in range(9):
            share(piece, slot).wait_send()


def on_device(n_ctx, n_head, queries, key_vectors, value_vectors, out_weight, offsets):
    rows, columns = queries.shape
    depth, features = out_weight.shape
    width = features // n_head
    dma = pltpu.SemaphoreType.DMA
    return pl.pallas_call(
        functools.partial(kernel, n_ctx, n_head),
        out_shape=jax.ShapeDtypeStruct((width, rows), jnp.bfloat16),
        in_specs=[pl.BlockSpec(memory_space=pltpu.SMEM)] + [pl.BlockSpec(memory_space=pl.ANY)] * 4,
        out_specs=pl.BlockSpec(memory_space=pltpu.VMEM),
        scratch_shapes=[
            pltpu.VMEM((9, 2, 2, rows, HEAD_DIM), jnp.bfloat16),
            pltpu.VMEM((rows, columns), jnp.bfloat16),
            pltpu.VMEM((n_head, depth, width), jnp.bfloat16),
            pltpu.VMEM((16, HEAD_DIM), jnp.int32),
            pltpu.VMEM((columns // HEAD_DIM, rows, 2 * HEAD_DIM), jnp.bfloat16),
            pltpu.VMEM((8, rows), jnp.float32),
            pltpu.VMEM((columns // HEAD_DIM, HEAD_DIM + 16, rows), jnp.float32),
            pltpu.VMEM((rows, columns), jnp.bfloat16),
            pltpu.VMEM((n_head, rows, width), jnp.float32),
            pltpu.VMEM((len(CHAINS), 4, rows // 4, width), jnp.bfloat16),
            pltpu.VMEM((len(CHAINS), 4, rows // 4, width), jnp.bfloat16),
            dma((3,)),
            dma((n_head,)),
            dma((2, 9, 9)),
            dma((2, 9)),
            dma((2, 9)),
            dma((2, 9)),
            dma((len(CHAINS), 4)),
            dma((len(CHAINS), 4)),
        ],
        compiler_params=pltpu.CompilerParams(
            collective_id=0, has_side_effects=True, vmem_limit_bytes=60 * 1024 * 1024
        ),
    )(offsets, queries, key_vectors, value_vectors, out_weight)


def solution(mesh):
    placed = (P("ctx", "head"), P("ctx", "head"), P("ctx", "head"), P("head", None), P())
    return jax.shard_map(
        functools.partial(on_device, mesh.shape["ctx"], mesh.shape["head"]),
        mesh=mesh,
        in_specs=placed,
        out_specs=P("head", "ctx"),
        check_vma=False,
    )
```
